512 devices in a mesh: ctx: 32 (over x, z), exp: 16 (over y, core).
Axes of the slice: x: 4, y: 8, z: 8, core: 2. Of those that a mesh axis runs over, the one named last changes fastest.
Arguments:
- tokens: bfloat16 [8192, 2880], P('ctx', 'exp'), may hold values from -6 to 6
- cotangent: bfloat16 [8192, 2880], P('ctx', 'exp'), may hold values from -4 to 4
- expert_indices: int32 [8192, 4], P('ctx'), may hold values from 0 to 127, all different within a row; in each aligned block of 256 rows (0 to 255, 256 to 511, ...) at most 16 rows name the same one
- routing_weights: float32 [8192, 4], P('ctx'), may hold values from 0.2 to 1
- gate_up_weight_blocks: bfloat16 [32, 2, 2880, 2880], P('ctx', None, 'exp'), may hold values from -6 to 6
- gate_up_block_scales: float32 [32, 2, 2880, 90], P('ctx', None, 'exp'), may hold values from 0.01 to 0.1
- down_weight_blocks: bfloat16 [32, 2880, 2880], P('ctx', 'exp'), may hold values from -6 to 6
- down_block_scales: float32 [32, 2880, 90], P('ctx', 'exp'), may hold values from 0.002 to 0.008
- adapter_down_matrix: bfloat16 [32, 2880, 16], P('ctx', 'exp'), may hold values from -0.109375 to 0.109375
- adapter_up_matrix: bfloat16 [32, 16, 2880], P('ctx', None, 'exp'), may hold values from -1.5 to 1.5
Outputs:
- moe_out: bfloat16 [8192, 2880], P('ctx', 'exp')
- left_gradient: float32 [32, 2880, 16], P('ctx', 'exp')
- right_gradient: float32 [32, 16, 2880], P('ctx', None, 'exp')
The draws below stay inside these ranges and needn't reach their ends.
Inputs may be any that keep to these rules, and one draw needn't show every extreme that they name: `expert_indices`: each row names 4 different experts. Within the 256 rows of one index of ctx no expert is named more than 16 times, a bound that some block reaches.
All inputs are finite; a program needn't handle non-finite values.
Results may differ from the reference program's by a relative error of at most 0.018.
Values may be sent and summed in bfloat16 or wider, within the bound.
No kernel may reach another device: no remote copies, remote signals or barrier semaphores. Data moves between devices by JAX's collectives and lax.ppermute only.
A program may use at most 64 MiB of HBM per device.

```python
import math
from functools import partial
import jax
import jax.numpy as jnp
import numpy as np
from jax import lax

MODEL_WIDTH = 2880
HIDDEN_UNITS = 2880
EXPERTS = 128
TOP = 4
ADAPTER_RANK = 16
TOK_DEV = 256
TOKENS = 8192
CAP = 16
EXPERTS_ACTIVE = 32
N_CTX = 32
N_EXP = 16


def spiked(entries, key, source, target, shards_of, factor):
    def block_of(axis_at):
        return (jnp.arange(entries.shape[axis_at]) // (entries.shape[axis_at] // shards_of)).reshape((-1,) + (1,) * (entries.ndim - 1 - axis_at))

    one_side = jax.random.permutation(key, shards_of)[block_of(target)]
    second = (block_of(target) + shards_of // 2) % shards_of
    return jnp.where((block_of(source) == one_side) | (block_of(source) == second), factor * entries, entries)


def steps_of(stream_key, extent, cuts, low, high):
    def one(axis_at, parts):
        steps = jax.random.uniform(jax.random.fold_in(jax.random.fold_in(stream_key, 6), axis_at), (parts,), jnp.float32, low / len(cuts), high / len(cuts))
        return jnp.repeat(jnp.exp(steps), extent[axis_at] // parts).reshape((-1,) + (1,) * (len(extent) - axis_at - 1))

    factor_of = one(*cuts[0])
    for cut in cuts[1:]:
        factor_of = factor_of * one(*cut)
    return factor_of


def assign_block(stream_key, own, number, rows, number_of, top, limit, slope):
    ranking = jax.random.permutation(stream_key, number_of)
    crowded, usual = load_shares(number_of, rows * top, limit, slope, True), load_shares(number_of, rows * top, limit, slope, False)
    places = jnp.arange(number_of)

    def named(tallies, turn):
        used = int((tallies > 0).sum())
        fixed = max(1, used // 4)
        moved = fixed + (places - fixed + turn * (used - fixed)) % max(1, number_of - fixed)
        return jnp.zeros((number_of,), jnp.int32).at[ranking[jnp.where(places < fixed, places, moved)]].set(jnp.asarray(tallies, jnp.int32))

    tallies = jnp.where(number % 4 == 0, named(crowded, number // 4), named(usual, number - number // 4 - 1))
    mixed = jax.random.permutation(jax.random.fold_in(own, 3), number_of)
    source_of, taker = mixed[0:number_of // 2 * 2:2], mixed[1:number_of // 2 * 2:2]
    margin = jnp.minimum(tallies[source_of] - 1, limit - tallies[taker]) // 2
    margin = jnp.where((source_of == ranking[0]) | (taker == ranking[0]) | (tallies[taker] == 0), 0, jnp.maximum(margin, 0))
    moved = jax.random.randint(jax.random.fold_in(own, 4), (number_of // 2,), 0, 1 << 20) % (margin + 1)
    tallies = tallies.at[source_of].add(-moved).at[taker].add(moved)
    members = jnp.searchsorted(jnp.cumsum(tallies), jnp.arange(rows * top), side="right").astype(jnp.int32)
    grid = members.reshape(top, rows).T
    grid = grid[jax.random.permutation(jax.random.fold_in(own, 1), rows)]
    turn = jax.random.randint(jax.random.fold_in(own, 2), (rows, 1), 0, top)
    return jnp.take_along_axis(grid, (jnp.arange(top)[None, :] + turn) % top, axis=1)


def load_shares(number_of, total, limit, slope, full):
    loads = [(1 << 20) // math.isqrt(standing ** slope) + 1 for standing in range(1, number_of + 1)]
    largest = limit if full else min(limit, max(-(-total // number_of), total * loads[0] // sum(loads)))
    least = 1 if total - largest >= number_of - 1 else 0
    counts, surplus = [largest] + [least] * (number_of - 1), total - largest - least * (number_of - 1)
    while surplus > 0:
        movable = [i for i in range(1, number_of) if counts[i] < largest] or [i for i in range(1, number_of) if counts[i] < limit]
        mass, budget = sum([loads[i] for i in movable]), surplus
        for i in movable:
            addition = min(limit - counts[i], max(1, budget * loads[i] // mass), surplus)
            counts[i] = counts[i] + addition
            surplus = surplus - addition
    return np.array(counts)


def normal_values(key, shape, scale, reach, cuts=(), kind=jnp.bfloat16):
    array = jax.random.normal(key, shape, jnp.float32) * scale
    if len(cuts) > 0:
        array = steps_of(key, shape, cuts, -0.22, 0.18) * array
    return jnp.clip(array, min=-reach, max=reach).astype(kind)


def noise_with(key, extent, scale, limit, shards, heavy, held_as=jnp.bfloat16):
    result = scale * jax.random.normal(key, extent, jnp.float32)
    if shards:
        result = result * steps_of(key, extent, shards, -0.22, 0.18)
    return jnp.clip(spiked(result, jax.random.fold_in(key, 3), *heavy), -limit, limit).astype(held_as)


def setup_inputs(seed: int = 0) -> dict:
    splits = jax.random.split(jax.random.key(seed), 11)
    tokens = normal_values(splits[0], (TOKENS, MODEL_WIDTH), 1.0, 6.0, ((0, 32), (1, 16)))
    cotangent = normal_values(splits[1], (TOKENS, MODEL_WIDTH), 0.25, 4.0, ((0, 32), (1, 16)))
    expert_indices_keys = jax.random.split(jax.random.fold_in(splits[2], 1), TOKENS // TOK_DEV)
    expert_indices_turns = jax.random.permutation(jax.random.fold_in(splits[2], 3), TOKENS // TOK_DEV)
    expert_indices = jax.vmap(lambda own, number: assign_block(jax.random.fold_in(splits[2], 2), own, number, TOK_DEV, EXPERTS, TOP, CAP, 2))(expert_indices_keys, expert_indices_turns).reshape((TOKENS, TOP))
    routing_weights = jnp.clip(0.2 + 0.8 * jax.random.uniform(splits[3], (TOKENS, TOP), jnp.float32) ** steps_of(splits[3], (TOKENS, TOP), ((0, 32),), -0.2, 0.2), 0.2, 1.0)
    gate_up_weight_blocks = normal_values(splits[4], (EXPERTS_ACTIVE, 2, HIDDEN_UNITS, MODEL_WIDTH), 1.0, 6.0, ((0, 32), (2, 16)))
    gate_up_block_scales = jnp.clip(jnp.exp(math.log(0.1) - 2.3025851 * jax.random.uniform(splits[5], (EXPERTS_ACTIVE, 2, HIDDEN_UNITS, MODEL_WIDTH // 32), jnp.float32) ** steps_of(splits[5], (EXPERTS_ACTIVE, 2, HIDDEN_UNITS, MODEL_WIDTH // 32), ((0, 32), (2, 16)), -0.2, 0.2)), 0.01, 0.1)
    down_weight_blocks = noise_with(splits[6], (EXPERTS_ACTIVE, HIDDEN_UNITS, MODEL_WIDTH), 1.0, 6.0, ((0, 32), (1, 16)), (1, 2, 16, 2.0))
    down_block_scales = jnp.clip(jnp.exp(math.log(0.008) - 1.3862944 * jax.random.uniform(splits[7], (EXPERTS_ACTIVE, HIDDEN_UNITS, MODEL_WIDTH // 32), jnp.float32) ** steps_of(splits[7], (EXPERTS_ACTIVE, HIDDEN_UNITS, MODEL_WIDTH // 32), ((0, 32), (1, 16)), -0.2, 0.2)), 0.002, 0.008)
    adapter_down_matrix = normal_values(splits[8], (EXPERTS_ACTIVE, HIDDEN_UNITS, ADAPTER_RANK), HIDDEN_UNITS ** -0.5, 0.109375, ((0, 32), (1, 16)))
    adapter_up_matrix = normal_values(splits[9], (EXPERTS_ACTIVE, ADAPTER_RANK, MODEL_WIDTH), ADAPTER_RANK ** -0.5, 1.5, ((0, 32), (2, 16)))
    return dict(tokens=tokens, cotangent=cotangent, expert_indices=expert_indices, routing_weights=routing_weights, gate_up_weight_blocks=gate_up_weight_blocks, gate_up_block_scales=gate_up_block_scales, down_weight_blocks=down_weight_blocks, down_block_scales=down_block_scales, adapter_down_matrix=adapter_down_matrix, adapter_up_matrix=adapter_up_matrix)


ADAPTER_SCALE = 0.5
GLU_ALPHA = 1.702
CLAMP_LIMIT = 7.0


def slot_table(expert_indices, flight, capacity):
    flat_ids = expert_indices.reshape(-1)
    onehot = (flat_ids[:, None] == jnp.arange(flight, dtype=jnp.int32)[None, :]).astype(jnp.int32)
    before = jnp.cumsum(onehot, axis=0) - onehot
    position = jnp.sum(before * onehot, axis=1)
    is_live = jnp.sum(onehot, axis=1) > 0
    target = jnp.where(is_live, flat_ids * capacity + position, -1)
    return target.reshape(expert_indices.shape).astype(jnp.int32)


def slot_sources(target, slot_count):
    flat_target = target.reshape(-1)
    matches = flat_target[None, :] == jnp.arange(slot_count, dtype=jnp.int32)[:, None]
    pair_index = jnp.arange(flat_target.shape[0], dtype=jnp.int32)
    chosen = jnp.sum(jnp.where(matches, pair_index[None, :], 0), axis=1).astype(jnp.int32)
    filled = jnp.any(matches, axis=1)
    return chosen, filled


def dispatch_rows(tokens, cotangent, routing_weights, chosen, filled, choices):
    token_of = chosen // choices
    weight_of = jnp.where(filled, routing_weights.reshape(-1)[chosen], 0.0)
    row_data = jnp.where(filled[:, None], tokens[token_of], jnp.zeros((), tokens.dtype))
    gradient_rows = (weight_of[:, None] * cotangent[token_of].astype(jnp.float32)).astype(jnp.bfloat16)
    return row_data, gradient_rows


def combine_rows(table, target, routing_weights):
    safe_index = jnp.maximum(target, 0).reshape(-1)
    picked = table[safe_index].astype(jnp.float32).reshape(target.shape + (table.shape[1],))
    scaled = jnp.where(target >= 0, routing_weights, 0.0)
    return jnp.sum(picked * scaled[:, :, None], axis=1).astype(jnp.bfloat16)


def dequant_gate_up(blocks, scales):
    pair, hidden, width = blocks.shape
    shaped = blocks.astype(jnp.float32).reshape(pair, hidden, width // 32, 32)
    return (shaped * scales[:, :, :, None]).reshape(pair, hidden, width).astype(jnp.bfloat16)


def dequant_down(blocks, scales):
    hidden, width = blocks.shape
    shaped = blocks.astype(jnp.float32).reshape(hidden, width // 32, 32)
    return (shaped * scales[:, :, None]).reshape(hidden, width).astype(jnp.bfloat16)


def glu_activate(gate_part, up_part):
    gate_cut = jnp.minimum(gate_part, CLAMP_LIMIT)
    up_cut = jnp.clip(up_part, -CLAMP_LIMIT, CLAMP_LIMIT)
    return ((up_cut + 1.0) * gate_cut * jax.nn.sigmoid(GLU_ALPHA * gate_cut)).astype(jnp.bfloat16)


def expert_update(operands):
    row_data, gradient_rows, joined_blocks, joined_scales, down_codes, down_factors, adapter_left, adapter_right = operands
    w_joined = dequant_gate_up(joined_blocks, joined_scales)
    w_down = dequant_down(down_codes, down_factors)
    hidden = w_down.shape[0]
    gate_part = jnp.dot(row_data, w_joined[0].T, preferred_element_type=jnp.float32)
    up_part = jnp.dot(row_data, w_joined[1].T, preferred_element_type=jnp.float32)
    activated = glu_activate(gate_part, up_part)
    width_part = hidden // N_EXP
    partial_sums = jnp.einsum("sgh,ghd->gsd", activated.reshape(-1, N_EXP, width_part).astype(jnp.float32), w_down.reshape(N_EXP, width_part, MODEL_WIDTH).astype(jnp.float32))
    rounded = lax.optimization_barrier(partial_sums.astype(jnp.bfloat16))
    frozen_base = jnp.sum(rounded.astype(jnp.float32), axis=0)
    reduced_rank = jnp.dot(activated, adapter_left, preferred_element_type=jnp.float32).astype(jnp.bfloat16)
    expert_output = (frozen_base + ADAPTER_SCALE * jnp.dot(reduced_rank, adapter_right, preferred_element_type=jnp.float32)).astype(jnp.bfloat16)
    right_gradient = ADAPTER_SCALE * jnp.dot(reduced_rank.T, gradient_rows, preferred_element_type=jnp.float32)
    backward_rank = (ADAPTER_SCALE * jnp.dot(gradient_rows, adapter_right.T, preferred_element_type=jnp.float32)).astype(jnp.bfloat16)
    left_gradient = jnp.dot(activated.T, backward_rank, preferred_element_type=jnp.float32)
    return expert_output, left_gradient, right_gradient


def reference(tokens, cotangent, expert_indices, routing_weights, gate_up_weight_blocks, gate_up_block_scales, down_weight_blocks, down_block_scales, adapter_down_matrix, adapter_up_matrix):
    flight = N_CTX
    slot_count = flight * CAP
    id_blocks = expert_indices.reshape(flight, TOK_DEV, TOP)
    weight_blocks = routing_weights.reshape(flight, TOK_DEV, TOP)
    token_blocks = tokens.reshape(flight, TOK_DEV, MODEL_WIDTH)
    cot_blocks = cotangent.reshape(flight, TOK_DEV, MODEL_WIDTH)
    targets = jax.vmap(partial(slot_table, flight=flight, capacity=CAP))(id_blocks)
    chosen, filled = jax.vmap(partial(slot_sources, slot_count=slot_count))(targets)
    row_data, gradient_rows = jax.vmap(partial(dispatch_rows, choices=TOP))(token_blocks, cot_blocks, weight_blocks, chosen, filled)
    per_expert = row_data.reshape(flight, flight, CAP, MODEL_WIDTH).transpose(1, 0, 2, 3).reshape(flight, slot_count, MODEL_WIDTH)
    gradients_per = gradient_rows.reshape(flight, flight, CAP, MODEL_WIDTH).transpose(1, 0, 2, 3).reshape(flight, slot_count, MODEL_WIDTH)
    expert_output, left_gradient, right_gradient = lax.map(expert_update, (per_expert, gradients_per, gate_up_weight_blocks, gate_up_block_scales, down_weight_blocks, down_block_scales, adapter_down_matrix, adapter_up_matrix))
    tables = expert_output.reshape(flight, flight, CAP, MODEL_WIDTH).transpose(1, 0, 2, 3).reshape(flight, slot_count, MODEL_WIDTH)
    moe_out = jax.vmap(combine_rows)(tables, targets, weight_blocks).reshape(TOKENS, MODEL_WIDTH)
    return moe_out, left_gradient, right_gradient
```

```python
import jax
import jax.numpy as jnp
from jax import lax
from jax.experimental import pallas as pl
from jax.experimental.pallas import tpu as pltpu
from jax.sharding import PartitionSpec as P

CAP = 16
HALF = CAP // 2
ADAPTER_SCALE = 0.5
GLU_ALPHA = 1.702
CLAMP_LIMIT = 7.0
BF = jnp.bfloat16
F32 = jnp.float32


NN = (((1,), (0,)), ((), ()))
NT = (((1,), (1,)), ((), ()))
TN = (((0,), (0,)), ((), ()))


def dot(a, b, dims):
    return lax.dot_general(a, b, dims, preferred_element_type=F32)


def iota(shape, axis):
    return lax.broadcasted_iota(jnp.int32, shape, axis)


def call(body, out_shape, *args, scalars=1):
    specs = [pl.BlockSpec(memory_space=pltpu.SMEM)] * scalars
    specs += [pl.BlockSpec(memory_space=pltpu.VMEM)] * (len(args) - scalars)
    return pl.pallas_call(
        body,
        out_shape=out_shape,
        in_specs=specs,
        out_specs=jax.tree.map(lambda _: pl.BlockSpec(memory_space=pltpu.VMEM), out_shape),
        name=body.__name__,
    )(*args)


def shape(dims, kind):
    return jax.ShapeDtypeStruct(dims, kind)


def place(width, part, side):
    return jnp.where(
        iota((2 * width, width), 0) == iota((2 * width, width), 1) + side * width, 1.0, 0.0
    ).astype(BF)


def route_rows(where, ids, weights, tok, tok_far, cot, cot_far, rows, grads, pick, weigh):
    side = where[1]
    flight = rows.shape[0] // HALF
    count = ids.shape[1]
    width = tok.shape[0]
    named = jnp.zeros((flight, count), F32)
    weight = jnp.zeros((flight, count), F32)
    for k in range(ids.shape[0]):
        hit = ids[k : k + 1, :] == iota((flight, count), 0)
        named = named + jnp.where(hit, 1.0, 0.0)
        weight = weight + jnp.where(hit, weights[k : k + 1, :], 0.0)
    earlier = jnp.where(iota((count, count), 0) < iota((count, count), 1), 1.0, 0.0).astype(BF)
    before = dot(named.astype(BF), earlier, NN) - (side * HALF).astype(F32)
    slot = iota((flight, HALF, count), 1).astype(F32)
    taken = (before[:, None, :] == slot) & (named[:, None, :] > 0.5)
    chosen = jnp.where(taken, 1.0, 0.0).reshape(flight * HALF, count)
    scaled = jnp.where(taken, weight[:, None, :], 0.0).reshape(flight * HALF, count)
    one = chosen.astype(BF)
    upper = scaled.astype(BF)
    pick[...] = upper
    weigh[...] = (scaled - upper.astype(F32)).astype(BF)
    near = place(width, 0, side)
    far = place(width, 0, 1 - side)
    features = (dot(near, tok[...], NN) + dot(far, tok_far[...], NN)).astype(BF)
    rows[...] = dot(one, features, NT).astype(BF)
    features = (dot(near, cot[...], NN) + dot(far, cot_far[...], NN)).astype(BF)
    factor = jnp.sum(scaled, axis=1, keepdims=True)
    grads[...] = (factor * dot(one, features, NT)).astype(BF)


def prepare(where, joined, joined_scales, down, down_scales, left, out, out_down):
    chip = where[0]
    parts = out.shape[0]
    piece = out.shape[3]
    hidden = down.shape[0]
    groups = down_scales.shape[1]
    width = down.shape[1]
    group = width // groups
    spread = jnp.where(
        iota((groups, width), 1) // group == iota((groups, width), 0), 1.0, 0.0
    ).astype(BF)

    def scaled(codes, scales):
        upper = scales.astype(BF)
        lower = (scales - upper.astype(F32)).astype(BF)
        return codes.astype(F32) * (dot(upper, spread, NN) + dot(lower, spread, NN))

    for c in range(2):
        full = scaled(joined[c], joined_scales[c])
        for a in range(parts):
            q = lax.rem(a - chip + parts, parts)
            out[q, c] = full[:, a * piece : (a + 1) * piece].astype(BF)
    full = scaled(down[...], down_scales[...])
    pad = out_down.shape[2]
    tail = left[...]
    shifted = jnp.where(
        iota((tail.shape[0], pad), 1) == iota((tail.shape[0], pad), 0) + piece, 1.0, 0.0
    ).astype(BF)
    added = dot(tail, shifted, TN)
    for a in range(parts):
        q = lax.rem(a - chip + parts, parts)
        out_down[q] = added.astype(BF)
        out_down[q, :, :piece] = full[:, a * piece : (a + 1) * piece].astype(BF)
        out_down[q, :, piece:] = added[:, piece:].astype(BF)


def expert_in(
    near, far, x0, r1, l1, r2, l2, r3, l3, r4, l4, near_down, far_down, grads, up, act_near, act_far, up_half, down_half, back
):
    count = x0.shape[0]
    parts = near.shape[0]
    blocks = [x0, l1, l2, l3, None, r3, r2, r1]
    for weights, act in ((near, act_near), (far, act_far)):
        sums = []
        for c in range(2):
            acc = jnp.zeros((count, weights.shape[2]), F32)
            for q in range(parts):
                if blocks[q] is None:
                    continue
                acc = acc + dot(blocks[q][...], weights[q, c], NT)
            last = jnp.concatenate(
                [dot(r4[...], weights[parts // 2, c], NT), dot(l4[...], weights[parts // 2, c], NT)], axis=0
            )
            sums.append(acc + last)
        gate = jnp.minimum(sums[0], CLAMP_LIMIT)
        lift = jnp.clip(sums[1], -CLAMP_LIMIT, CLAMP_LIMIT)
        act[...] = ((lift + 1.0) * gate * jax.nn.sigmoid(GLU_ALPHA * gate)).astype(BF)
    mid = parts // 2
    total = dot(act_near[...], near_down[mid], NN) + dot(act_far[...], far_down[mid], NN)
    total = total.astype(BF)
    rank = up.shape[0]
    partial = dot(up[...], grads[...], NT).astype(BF)
    cut = up_half.shape[0]
    back[...] = jnp.zeros(back.shape, BF)
    back[:, :count] = partial
    up_half[...] = total[:cut]
    down_half[: count - cut] = total[cut:]
    down_half[count - cut :] = back[...]


def expert_out(act_near, act_far, near_down, far_down, back, out):
    count = act_near.shape[0]
    parts = near_down.shape[0]
    mid = parts // 2
    for i, q in enumerate([mid - 1, mid + 1, mid - 2, mid + 2, 1, parts - 1, 0]):
        total = dot(act_near[...], near_down[q], NN) + dot(act_far[...], far_down[q], NN)
        out[i, :count] = total.astype(BF)
        out[i, count:] = back[...]


def finish(own, fromlow, fromhigh, up, out, summed):
    count, piece = out.shape
    total = own[...].astype(F32) + fromlow[...].astype(F32) + fromhigh[...].astype(F32)
    rounded = total.astype(BF)
    summed[...] = rounded
    pad = total.shape[1]
    rank = up.shape[0]
    lift = jnp.where(iota((pad, rank), 0) == iota((pad, rank), 1) + piece, 1.0, 0.0).astype(BF)
    low = dot(rounded[:count], lift, NN).astype(BF)
    added = ADAPTER_SCALE * dot(low, up[...], NN)
    out[...] = (total[:count, :piece] + added).astype(BF)


def gradients(summed, act_near, act_far, grads, left_near, left_far, right):
    count, piece = grads.shape
    rank = left_near.shape[0]
    back = (ADAPTER_SCALE * summed[count:, :count].astype(F32)).astype(BF)
    left_near[...] = dot(back, act_near[...], NN)
    left_far[...] = dot(back, act_far[...], NN)
    product = dot(summed[:count, :], grads[...], TN)
    right[...] = ADAPTER_SCALE * product[piece : piece + rank]


def combine(returned, pick, weigh, out):
    out[...] = dot(returned[...], pick[...], TN) + dot(returned[...], weigh[...], TN)


def on_device(
    tokens,
    cotangent,
    expert_indices,
    routing_weights,
    gate_up_weight_blocks,
    gate_up_block_scales,
    down_weight_blocks,
    down_block_scales,
    adapter_down_matrix,
    adapter_up_matrix,
):
    flight = lax.axis_size("ctx")
    peers = lax.axis_size("exp")
    ring = peers // 2
    index = lax.axis_index("exp")
    chip, side = index // 2, index % 2
    where = jnp.stack([chip, side]).astype(jnp.int32)
    swap_pairs = [(i, i ^ 1) for i in range(peers)]

    def swap(x):
        return lax.ppermute(x, "exp", swap_pairs)

    def shift(x, by):
        return lax.ppermute(
            x, "exp", [(2 * y + c, 2 * ((y + by) % ring) + c) for y in range(ring) for c in range(2)]
        )

    tok, cot = tokens.T, cotangent.T
    width, count = tok.shape
    slots = flight * HALF
    hidden = down_weight_blocks.shape[1]
    model = down_weight_blocks.shape[2]
    piece = 2 * width
    rank = adapter_up_matrix.shape[1]
    pad = -(-(piece + rank) // 128) * 128
    tok_far, cot_far = swap(tok), swap(cot)
    up_near = adapter_up_matrix[0]
    up_far = swap(up_near)
    up = jnp.where(
        side == 0,
        jnp.concatenate([up_near, up_far], axis=1),
        jnp.concatenate([up_far, up_near], axis=1),
    )

    rows, grads, pick, weigh = call(
        route_rows,
        (
            shape((slots, piece), BF),
            shape((slots, piece), BF),
            shape((slots, count), BF),
            shape((slots, count), BF),
        ),
        where, expert_indices.T, routing_weights.T, tok, tok_far, cot, cot_far,
    )

    def trade(x):
        x = x.reshape(flight, HALF, piece)
        return lax.all_to_all(x, "ctx", split_axis=0, concat_axis=0, tiled=True).reshape(slots, piece)

    x0 = trade(rows)
    got_grads = trade(grads)

    near, near_down = call(
        prepare,
        (shape((ring, 2, hidden, piece), BF), shape((ring, hidden, pad), BF)),
        where,
        gate_up_weight_blocks[0],
        gate_up_block_scales[0],
        down_weight_blocks[0],
        down_block_scales[0],
        adapter_down_matrix[0].T,
    )
    far, far_down = swap(near), swap(near_down)

    r1, l1 = shift(x0, 1), shift(x0, -1)
    r2, l2 = shift(r1, 1), shift(l1, -1)
    r3, l3 = shift(r2, 1), shift(l2, -1)
    r4, l4 = shift(r3[: slots // 2], 1), shift(l3[slots // 2 :], -1)

    tall = slots + rank
    cut = tall // 2
    act_near, act_far, high, low, back = call(
        expert_in,
        (
            shape((slots, hidden), BF),
            shape((slots, hidden), BF),
            shape((cut, pad), BF),
            shape((tall - cut, pad), BF),
            shape((rank, pad), BF),
        ),
        near, far, x0, r1, l1, r2, l2, r3, l3, r4, l4, near_down, far_down, got_grads, up,
        scalars=0,
    )
    sums = call(
        expert_out, shape((ring - 1, tall, pad), BF), act_near, act_far, near_down, far_down, back, scalars=0
    )

    def add(a, b):
        return (a.astype(F32) + b.astype(F32)).astype(BF)

    up_sum = shift(high, 1)
    down_sum = shift(low, -1)
    up_sum = jnp.concatenate([add(up_sum, sums[0, :cut]), sums[0, cut:]], axis=0)
    down_sum = jnp.concatenate([sums[1, :cut], add(down_sum, sums[1, cut:])], axis=0)
    up_sum, down_sum = shift(up_sum, 1), shift(down_sum, -1)
    up_sum, down_sum = add(up_sum, sums[2]), add(down_sum, sums[3])
    up_sum, down_sum = shift(up_sum, 1), shift(down_sum, -1)
    up_sum, down_sum = add(up_sum, sums[4]), add(down_sum, sums[5])
    up_sum, down_sum = shift(up_sum, 1), shift(down_sum, -1)

    expert_rows, summed = call(
        finish,
        (shape((slots, piece), BF), shape((tall, pad), BF)),
        sums[6], up_sum, down_sum, up,
        scalars=0,
    )
    returned = trade(expert_rows)
    left_near, left_far, right = call(
        gradients,
        (shape((rank, hidden), F32), shape((rank, hidden), F32), shape((rank, piece), F32)),
        summed, act_near, act_far, got_grads,
        scalars=0,
    )
    left = left_near + swap(left_far)

    def halves(x, axis):
        first, second = jnp.split(x, 2, axis=axis)
        mine = jnp.where(side == 0, first, second)
        other = jnp.where(side == 0, second, first)
        return mine, other

    right_mine, right_other = halves(right, 1)
    right_out = right_mine + swap(right_other)
    moe = call(combine, shape((piece, count), F32), returned, pick, weigh, scalars=0)
    moe_mine, moe_other = halves(moe, 0)
    moe_out = (moe_mine + swap(moe_other)).astype(BF).T
    return (moe_out, left.T[None], right_out[None])


def solution(mesh):
    placed = (
        P("ctx", "exp"),
        P("ctx", "exp"),
        P("ctx", None),
        P("ctx", None),
        P("ctx", None, "exp", None),
        P("ctx", None, "exp", None),
        P("ctx", "exp", None),
        P("ctx", "exp", None),
        P("ctx", "exp", None),
        P("ctx", None, "exp"),
    )
    return jax.shard_map(
        on_device,
        mesh=mesh,
        in_specs=placed,
        out_specs=(P("ctx", "exp"), P("ctx", "exp", None), P("ctx", None, "exp")),
        check_vma=False,
    )
```

```python
import jax
import jax.numpy as jnp
from jax import lax
from jax.experimental import pallas as pl
from jax.experimental.pallas import tpu as pltpu
from jax.sharding import PartitionSpec as P


CAP = 16
HALF = CAP // 2
ADAPTER_SCALE = 0.5
GLU_ALPHA = 1.702
CLAMP_LIMIT = 7.0
BF = jnp.bfloat16
F32 = jnp.float32


NN = (((1,), (0,)), ((), ()))
NT = (((1,), (1,)), ((), ()))
TN = (((0,), (0,)), ((), ()))

ORDER = (0, 1, -1, -2, 2, 3, -3, -4)


def dot(a, b, dims):
    return lax.dot_general(a, b, dims, preferred_element_type=F32)


def iota(shape, axis):
    return lax.broadcasted_iota(jnp.int32, shape, axis)


def up8(n):
    return -(-n // 8) * 8


def up128(n):
    return -(-n // 128) * 128


def call(body, out_shape, *args, scalars=1, keep=False, local=(), scratch=()):
    smem = pl.BlockSpec(memory_space=pltpu.SMEM)
    vmem = pl.BlockSpec(memory_space=pltpu.VMEM)
    args = [
        pltpu.with_memory_space_constraint(x, pltpu.VMEM) if i in local else x
        for i, x in enumerate(args)
    ]
    return pl.pallas_call(
        body,
        out_shape=[
            pltpu.VMEM(dims, kind) if keep else pltpu.HBM(dims, kind) for dims, kind in out_shape
        ],
        in_specs=[smem if i < scalars else vmem for i in range(len(args))],
        out_specs=[vmem for _ in out_shape],
        scratch_shapes=list(scratch),
        compiler_params=pltpu.CompilerParams(vmem_limit_bytes=24 << 20),
    )(*args)


def route_rows(where, ids, weights, near, far, rows, grads, pick, weigh):
    side = where[1]
    flight = rows.shape[0] // HALF
    count = ids.shape[1]
    both = near.shape[0]
    width = both // 2
    named = jnp.zeros((flight, count), F32)
    weight = jnp.zeros((flight, count), F32)
    for k in range(ids.shape[0]):
        hit = ids[k : k + 1, :] == iota((flight, count), 0)
        named = named + jnp.where(hit, 1.0, 0.0)
        weight = weight + jnp.where(hit, weights[k : k + 1, :], 0.0)
    earlier = jnp.where(iota((count, count), 0) < iota((count, count), 1), 1.0, 0.0).astype(BF)
    before = dot(named.astype(BF), earlier, NN) - (side * HALF).astype(F32)
    slot = iota((flight, HALF, count), 1).astype(F32)
    taken = (before[:, None, :] == slot) & (named[:, None, :] > 0.5)
    chosen = jnp.where(taken, 1.0, 0.0).reshape(flight * HALF, count)
    scaled = jnp.where(taken, weight[:, None, :], 0.0).reshape(flight * HALF, count)
    one = chosen.astype(BF)
    upper = scaled.astype(BF)
    pick[...] = upper
    weigh[...] = (scaled - upper.astype(F32)).astype(BF)
    row, col = iota((both, both), 0), iota((both, both), 1)

    def features(second):
        inside = (col >= width) if second else (col < width)
        at = row + width if second else row
        left = (at == col + side * width) & inside
        right = (at == col + (1 - side) * width) & inside
        left = jnp.where(left, 1.0, 0.0).astype(BF)
        right = jnp.where(right, 1.0, 0.0).astype(BF)
        return (dot(left, near[...], NN) + dot(right, far[...], NN)).astype(BF)

    rows[...] = dot(one, features(False), NT).astype(BF)
    factor = jnp.sum(scaled, axis=1, keepdims=True)
    grads[...] = (factor * dot(one, features(True), NT)).astype(BF)


def prepare(joined, joined_scales, down, down_scales, left, up, out):
    hidden, width = down.shape
    groups = down_scales.shape[1]
    group = width // groups
    parts = len(ORDER)
    piece = width // parts
    rank = left.shape[0]
    pad = out.shape[2]
    spread = jnp.where(
        iota((groups, width), 1) // group == iota((groups, width), 0), 1.0, 0.0
    ).astype(BF)

    def scaled(codes, scales):
        upper = scales.astype(BF)
        lower = (scales - upper.astype(F32)).astype(BF)
        return codes.astype(F32) * (dot(upper, spread, NN) + dot(lower, spread, NN))

    for c in range(2):
        full = scaled(joined[c], joined_scales[c])
        for a in range(parts):
            out[2 * a + c, :hidden, :piece] = full[:, a * piece : (a + 1) * piece].astype(BF)
    full = scaled(down[...], down_scales[...])
    shifted = jnp.where(iota((rank, pad), 1) == iota((rank, pad), 0) + piece, 1.0, 0.0).astype(BF)
    added = dot(left[...], shifted, TN).astype(BF)
    for a in range(parts):
        out[2 * parts + a, :hidden, :] = added
        out[2 * parts + a, :hidden, :piece] = full[:, a * piece : (a + 1) * piece].astype(BF)
    out[3 * parts, :rank, : up.shape[1]] = up[...]


def source(where, q):
    parts = len(ORDER)
    return lax.rem(where[0] + where[2] * ORDER[q] + parts, parts)


def project_into(where, first, near, far, blocks, before, sums):
    hidden, count = sums.shape[3], sums.shape[2]
    piece = blocks[0].shape[1]
    spans = [(x, h * count) for x in blocks for h in range(2)]
    for n, weights in enumerate((near, far)):
        for c in range(2):
            acc = jnp.zeros((count, hidden), F32) if before is None else before[n, c]
            for q, (x, at) in enumerate(spans):
                part = weights[2 * source(where, first + q) + c, :hidden, :piece]
                acc = acc + dot(x[at : at + count, :], part, NT)
            sums[n, c] = acc


def project_four(where, near, far, first, second, sums):
    project_into(where, 0, near, far, (first, second), None, sums)


def project_more(where, near, far, third, before, sums):
    project_into(where, 4, near, far, (third,), before, sums)


def expert(where, near, far, sums, last, grads, act_near, act_far, up, out, wide):
    side = where[1]
    count, hidden = act_near.shape
    piece = last.shape[1]
    parts = len(ORDER)
    rank = up.shape[0]
    half = piece // 2
    tall = out.shape[0] // parts
    pad = out.shape[1]
    acts = []
    for n, (weights, act) in enumerate(((near, act_near), (far, act_far))):
        total = []
        for c in range(2):
            acc = sums[n, c]
            for h in range(2):
                part = weights[2 * source(where, parts - 2 + h) + c, :hidden, :piece]
                acc = acc + dot(last[h * count : (h + 1) * count, :], part, NT)
            total.append(acc)
        gate = jnp.minimum(total[0], CLAMP_LIMIT)
        lift = jnp.clip(total[1], -CLAMP_LIMIT, CLAMP_LIMIT)
        value = ((lift + 1.0) * gate * jax.nn.sigmoid(GLU_ALPHA * gate)).astype(BF)
        act[...] = value
        acts.append(value)
    row, col = iota((half, piece), 0), iota((half, piece), 1)
    here = jnp.where(row + side * half == col, 1.0, 0.0).astype(BF)
    there = jnp.where(row + (1 - side) * half == col, 1.0, 0.0).astype(BF)
    both = dot(near[3 * parts, :rank, :half], here, NN) + dot(far[3 * parts, :rank, :half], there, NN)
    both = both.astype(BF)
    up[...] = both
    back = dot(both, grads[...], NT)
    for a in range(parts):
        total = dot(acts[0], near[2 * parts + a, :hidden, :], NN) + dot(acts[1], far[2 * parts + a, :hidden, :], NN)
        wide[a * tall : a * tall + count, :] = total
        wide[a * tall + count : (a + 1) * tall, :] = jnp.zeros((tall - count, pad), F32)
        wide[a * tall + count : a * tall + count + rank, :count] = back
    out[...] = wide[...].astype(BF)


def finish(total, up, out):
    count, piece = out.shape
    pad = total.shape[1]
    rank = up.shape[0]
    lift = jnp.where(iota((pad, rank), 0) == iota((pad, rank), 1) + piece, 1.0, 0.0).astype(BF)
    low = dot(total[:count, :], lift, NN).astype(BF)
    added = ADAPTER_SCALE * dot(low, up[...], NN)
    out[...] = (total[:count, :piece].astype(F32) + added).astype(BF)


def gradients(where, total, act_near, act_far, grads, left, right, send):
    side = where[1]
    count, piece = grads.shape
    rank, half = left.shape
    back = (ADAPTER_SCALE * total[count : count + rank, :count].astype(F32)).astype(BF)
    left[...] = dot(back, act_near[...], NN)
    product = dot(total[:count, :], grads[...], TN)
    whole = ADAPTER_SCALE * product[piece : piece + rank]
    first, second = whole[:, :half], whole[:, half:]
    right[...] = jnp.where(side == 0, first, second)
    send[...] = jnp.zeros(send.shape, F32)
    send[:rank, :half] = dot(back, act_far[...], NN)
    send[rank:, :half] = jnp.where(side == 0, second, first)


def combine(where, returned, pick, weigh, ranks, mine, send, whole):
    side = where[1]
    half = mine.shape[0]
    whole[...] = dot(returned[...], pick[...], TN) + dot(returned[...], weigh[...], TN)
    first, second = whole[:half, :], whole[half:, :]
    mine[...] = jnp.where(side == 0, first, second)
    send[:half, :] = jnp.where(side == 0, second, first)
    start = send.shape[0] - ranks.shape[0]
    send[start:, :] = ranks[...]


def settle(mine, left, right, got, out, left_out, right_out):
    half = mine.shape[0]
    rank, wide = left.shape
    start = got.shape[0] - 2 * rank
    out[...] = (mine[...] + got[:half, :]).astype(BF)
    left_out[...] = left[...] + got[start : start + rank, :wide]
    right_out[...] = right[...] + got[start + rank :, :wide]


def on_device(
    tokens,
    cotangent,
    expert_indices,
    routing_weights,
    gate_up_weight_blocks,
    gate_up_block_scales,
    down_weight_blocks,
    down_block_scales,
    adapter_down_matrix,
    adapter_up_matrix,
):
    flight = lax.axis_size("ctx")
    peers = lax.axis_size("exp")
    ring = peers // 2
    index = lax.axis_index("exp")
    chip, side = index // 2, index % 2
    sign = 1 - 2 * ((chip + side) % 2)
    where = jnp.stack([chip, side, sign]).astype(jnp.int32)
    swap_pairs = [(i, i ^ 1) for i in range(peers)]

    def swap(x):
        return lax.ppermute(x, "exp", swap_pairs)

    def trade_along(x, step):
        pairs = []
        for y in range(ring):
            for c in range(2):
                way = step if (y + c) % 2 == 0 else -step
                pairs.append((2 * y + c, 2 * ((y + way) % ring) + c))
        return lax.ppermute(x, "exp", pairs)

    width, count = tokens.shape[1], tokens.shape[0]
    slots = flight * HALF
    hidden, _ = down_weight_blocks.shape[1:]
    piece = 2 * width
    rank = adapter_up_matrix.shape[1]
    pad = up128(piece + rank)

    own = jnp.concatenate([tokens.T, cotangent.T], axis=0)
    other = swap(own)
    rows, grads, pick, weigh = call(
        route_rows,
        [((slots, piece), BF)] * 2 + [((slots, count), BF)] * 2,
        where, expert_indices.T, routing_weights.T, own, other,
        local=(3, 4),
    )

    def trade(x):
        x = x.reshape(flight, HALF, piece)
        return lax.all_to_all(x, "ctx", split_axis=0, concat_axis=0, tiled=True).reshape(slots, piece)

    x0 = trade(rows)
    got_grads = trade(grads)

    (near,) = call(
        prepare,
        [((3 * ring + 1, up8(hidden), pad), BF)],
        gate_up_weight_blocks[0],
        gate_up_block_scales[0],
        down_weight_blocks[0],
        down_block_scales[0],
        adapter_down_matrix[0].T,
        adapter_up_matrix[0],
        scalars=0, keep=True,
    )
    far = swap(near)

    x1 = trade_along(x0, 1)
    first = jnp.concatenate([x0, x1], axis=0)
    second = trade_along(first, -1)
    third = trade_along(second, 1)
    last = trade_along(third, -1)
    (sums,) = call(
        project_four, [((2, 2, slots, hidden), F32)], where, near, far, first, second, local=(1, 2)
    )
    (sums,) = call(
        project_more, [((2, 2, slots, hidden), F32)], where, near, far, third, sums, local=(1, 2)
    )
    tall = slots + rank + 4
    act_near, act_far, up, partial = call(
        expert,
        [((slots, hidden), BF)] * 2 + [((rank, piece), BF), ((ring * tall, pad), BF)],
        where, near, far, sums, last, got_grads,
        local=(1, 2, 4),
        scratch=[pltpu.VMEM((ring * tall, pad), F32)],
    )
    groups = [[2 * y + c for y in range(ring)] for c in range(2)]
    total = lax.psum_scatter(
        partial, "exp", scatter_dimension=0, tiled=True, axis_index_groups=groups
    )
    (expert_rows,) = call(finish, [((slots, piece), BF)], total, up, scalars=0, local=(0,))
    returned = trade(expert_rows)
    left, right, ranks = call(
        gradients,
        [((rank, hidden), F32), ((rank, width), F32), ((2 * rank, count), F32)],
        where, total, act_near, act_far, got_grads,
        keep=True, local=(1,),
    )
    mine, send = call(
        combine,
        [((width, count), F32), ((up8(width) + 2 * rank, count), F32)],
        where, returned, pick, weigh, ranks,
        keep=True, local=(1, 4),
        scratch=[pltpu.VMEM((piece, count), F32)],
    )
    got = swap(send)
    moe, left, right = call(
        settle,
        [((width, count), BF), ((rank, hidden), F32), ((rank, width), F32)],
        mine, left, right, got,
        scalars=0, local=(0, 1, 2, 3),
    )
    return (moe.T, left.T[None], right[None])


def solution(mesh):
    placed = (
        P("ctx", "exp"),
        P("ctx", "exp"),
        P("ctx", None),
        P("ctx", None),
        P("ctx", None, "exp", None),
        P("ctx", None, "exp", None),
        P("ctx", "exp", None),
        P("ctx", "exp", None),
        P("ctx", "exp", None),
        P("ctx", None, "exp"),
    )
    return jax.shard_map(
        on_device,
        mesh=mesh,
        in_specs=placed,
        out_specs=(P("ctx", "exp"), P("ctx", "exp", None), P("ctx", None, "exp")),
        check_vma=False,
    )
```

```python
import jax
import jax.numpy as jnp
from jax import lax
from jax.experimental import pallas as pl
from jax.experimental.pallas import tpu as pltpu
from jax.sharding import PartitionSpec as P


CAP = 16
HALF = CAP // 2
ADAPTER_SCALE = 0.5
GLU_ALPHA = 1.702
CLAMP_LIMIT = 7.0
BF = jnp.bfloat16
F32 = jnp.float32


NN = (((1,), (0,)), ((), ()))
NT = (((1,), (1,)), ((), ()))
TN = (((0,), (0,)), ((), ()))

ORDER = (0, 1, -1, -2, 2, 3, -3, -4)


def dot(a, b, dims):
    return lax.dot_general(a, b, dims, preferred_element_type=F32)


def iota(shape, axis):
    return lax.broadcasted_iota(jnp.int32, shape, axis)


def up8(n):
    return -(-n // 8) * 8


def up128(n):
    return -(-n // 128) * 128


def call(body, out_shape, *args, scalars=1, keep=False, local=(), free=(), scratch=()):
    smem = pl.BlockSpec(memory_space=pltpu.SMEM)
    vmem = pl.BlockSpec(memory_space=pltpu.VMEM)
    args = [
        x
        if i < scalars or i in free
        else pltpu.with_memory_space_constraint(x, pltpu.VMEM if i in local else pltpu.HBM)
        for i, x in enumerate(args)
    ]
    return pl.pallas_call(
        body,
        out_shape=[
            pltpu.VMEM(dims, kind) if keep else pltpu.HBM(dims, kind) for dims, kind in out_shape
        ],
        in_specs=[smem if i < scalars else vmem for i in range(len(args))],
        out_specs=[vmem for _ in out_shape],
        scratch_shapes=list(scratch),
        compiler_params=pltpu.CompilerParams(vmem_limit_bytes=24 << 20),
    )(*args)


def assign(where, ids, weights, pick, weigh, one):
    side = where[1]
    slots, count = pick.shape
    flight = slots // HALF
    named = jnp.zeros((flight, count), F32)
    weight = jnp.zeros((flight, count), F32)
    for k in range(ids.shape[0]):
        hit = ids[k : k + 1, :] == iota((flight, count), 0)
        named = named + jnp.where(hit, 1.0, 0.0)
        weight = weight + jnp.where(hit, weights[k : k + 1, :], 0.0)
    earlier = jnp.where(iota((count, count), 0) < iota((count, count), 1), 1.0, 0.0).astype(BF)
    before = dot(named.astype(BF), earlier, NN) - (side * HALF).astype(F32)
    slot = iota((flight, HALF, count), 1).astype(F32)
    taken = (before[:, None, :] == slot) & (named[:, None, :] > 0.5)
    one[...] = jnp.where(taken, 1.0, 0.0).reshape(slots, count).astype(BF)
    scaled = jnp.where(taken, weight[:, None, :], 0.0).reshape(slots, count)
    upper = scaled.astype(BF)
    pick[...] = upper
    weigh[...] = (scaled - upper.astype(F32)).astype(BF)


def features(where, near, far):
    side = where[1]
    width = near.shape[0]
    row, col = iota((2 * width, width), 0), iota((2 * width, width), 1)
    left = jnp.where(row == col + side * width, 1.0, 0.0).astype(BF)
    right = jnp.where(row == col + (1 - side) * width, 1.0, 0.0).astype(BF)
    return (dot(left, near[...], NN) + dot(right, far[...], NN)).astype(BF)


def select_rows(where, one, near, far, rows):
    rows[...] = dot(one[...], features(where, near, far), NT).astype(BF)


def select_grads(where, one, pick, weigh, near, far, grads):
    factor = jnp.sum(pick[...].astype(F32) + weigh[...].astype(F32), axis=1, keepdims=True)
    grads[...] = (factor * dot(one[...], features(where, near, far), NT)).astype(BF)


def join(first, second, out):
    count = first.shape[0]
    out[:count, :] = first[...]
    out[count:, :] = second[...]


def prepare(joined, joined_scales, down, down_scales, left, up, out):
    hidden, width = down.shape
    groups = down_scales.shape[2]
    group = width // groups
    parts = len(ORDER)
    piece = width // parts
    rank = left.shape[0]
    pad = out.shape[2]
    spread = jnp.where(
        iota((groups, width), 1) // group == iota((groups, width), 0), 1.0, 0.0
    ).astype(BF)

    def scaled(codes, scales):
        upper = scales.astype(BF)
        lower = (scales - upper.astype(F32)).astype(BF)
        return codes.astype(F32) * (dot(upper, spread, NN) + dot(lower, spread, NN))

    for c in range(2):
        full = scaled(joined[:, c, :], joined_scales[:, c, :])
        for a in range(parts):
            out[2 * a + c, :hidden, :piece] = full[:, a * piece : (a + 1) * piece].astype(BF)
    full = scaled(down[...], down_scales[:, 0, :])
    shifted = jnp.where(iota((rank, pad), 1) == iota((rank, pad), 0) + piece, 1.0, 0.0).astype(BF)
    added = dot(left[...], shifted, TN).astype(BF)
    for a in range(parts):
        out[2 * parts + a, :hidden, :] = added
        out[2 * parts + a, :hidden, :piece] = full[:, a * piece : (a + 1) * piece].astype(BF)
    out[3 * parts, :rank, : up.shape[1]] = up[...]


def source(where, q):
    parts = len(ORDER)
    return lax.rem(where[0] + where[2] * ORDER[q] + parts, parts)


def project_into(where, first, near, far, blocks, before, sums):
    hidden, count = sums.shape[3], sums.shape[2]
    piece = blocks[0].shape[1]
    spans = [(x, h * count) for x in blocks for h in range(2)]
    for n, weights in enumerate((near, far)):
        for c in range(2):
            acc = jnp.zeros((count, hidden), F32) if before is None else before[n, c]
            for q, (x, at) in enumerate(spans):
                part = weights[2 * source(where, first + q) + c, :hidden, :piece]
                acc = acc + dot(x[at : at + count, :], part, NT)
            sums[n, c] = acc


def project_four(where, near, far, first, second, sums):
    project_into(where, 0, near, far, (first, second), None, sums)


def project_more(where, near, far, third, before, sums):
    project_into(where, 4, near, far, (third,), before, sums)


def expert(where, near, far, sums, last, grads, act_near, act_far, up, out, wide):
    side = where[1]
    count, hidden = act_near.shape
    piece = last.shape[1]
    parts = len(ORDER)
    rank = up.shape[0]
    half = piece // 2
    tall = out.shape[0] // parts
    pad = out.shape[1]
    acts = []
    for n, (weights, act) in enumerate(((near, act_near), (far, act_far))):
        total = []
        for c in range(2):
            acc = sums[n, c]
            for h in range(2):
                part = weights[2 * source(where, parts - 2 + h) + c, :hidden, :piece]
                acc = acc + dot(last[h * count : (h + 1) * count, :], part, NT)
            total.append(acc)
        gate = jnp.minimum(total[0], CLAMP_LIMIT)
        lift = jnp.clip(total[1], -CLAMP_LIMIT, CLAMP_LIMIT)
        value = ((lift + 1.0) * gate * jax.nn.sigmoid(GLU_ALPHA * gate)).astype(BF)
        act[...] = value
        acts.append(value)
    row, col = iota((half, piece), 0), iota((half, piece), 1)
    here = jnp.where(row + side * half == col, 1.0, 0.0).astype(BF)
    there = jnp.where(row + (1 - side) * half == col, 1.0, 0.0).astype(BF)
    both = dot(near[3 * parts, :rank, :half], here, NN) + dot(far[3 * parts, :rank, :half], there, NN)
    both = both.astype(BF)
    up[...] = both
    back = dot(both, grads[...], NT)
    for a in range(parts):
        total = dot(acts[0], near[2 * parts + a, :hidden, :], NN) + dot(acts[1], far[2 * parts + a, :hidden, :], NN)
        wide[a * tall : a * tall + count, :] = total
        wide[a * tall + count : (a + 1) * tall, :] = jnp.zeros((tall - count, pad), F32)
        wide[a * tall + count : a * tall + count + rank, :count] = back
    out[...] = wide[...].astype(BF)


def finish(total, up, out):
    count, piece = out.shape
    pad = total.shape[1]
    rank = up.shape[0]
    lift = jnp.where(iota((pad, rank), 0) == iota((pad, rank), 1) + piece, 1.0, 0.0).astype(BF)
    low = dot(total[:count, :], lift, NN).astype(BF)
    added = ADAPTER_SCALE * dot(low, up[...], NN)
    out[...] = (total[:count, :piece].astype(F32) + added).astype(BF)


def gradients(where, total, act_near, act_far, grads, left, right, send):
    side = where[1]
    count, piece = grads.shape
    rank, half = left.shape
    back = (ADAPTER_SCALE * total[count : count + rank, :count].astype(F32)).astype(BF)
    left[...] = dot(back, act_near[...], NN)
    product = dot(total[:count, :], grads[...], TN)
    whole = ADAPTER_SCALE * product[piece : piece + rank]
    first, second = whole[:, :half], whole[:, half:]
    right[...] = jnp.where(side == 0, first, second)
    send[...] = jnp.zeros(send.shape, F32)
    send[:rank, :half] = dot(back, act_far[...], NN)
    send[rank:, :half] = jnp.where(side == 0, second, first)


def combine(where, returned, pick, weigh, ranks, mine, send, whole):
    side = where[1]
    half = mine.shape[0]
    whole[...] = dot(returned[...], pick[...], TN) + dot(returned[...], weigh[...], TN)
    first, second = whole[:half, :], whole[half:, :]
    mine[...] = jnp.where(side == 0, first, second)
    send[:half, :] = jnp.where(side == 0, second, first)
    start = send.shape[0] - ranks.shape[0]
    send[start:, :] = ranks[...]


def settle(mine, left, right, got, out, left_out, right_out):
    half = mine.shape[0]
    rank, wide = left.shape
    start = got.shape[0] - 2 * rank
    out[...] = (mine[...] + got[:half, :]).astype(BF)
    left_out[...] = left[...] + got[start : start + rank, :wide]
    right_out[...] = right[...] + got[start + rank :, :wide]


def on_device(
    tokens,
    cotangent,
    expert_indices,
    routing_weights,
    gate_up_weight_blocks,
    gate_up_block_scales,
    down_weight_blocks,
    down_block_scales,
    adapter_down_matrix,
    adapter_up_matrix,
):
    flight = lax.axis_size("ctx")
    peers = lax.axis_size("exp")
    ring = peers // 2
    index = lax.axis_index("exp")
    chip, side = index // 2, index % 2
    sign = 1 - 2 * ((chip + side) % 2)
    where = jnp.stack([chip, side, sign]).astype(jnp.int32)
    swap_pairs = [(i, i ^ 1) for i in range(peers)]

    def swap(x):
        return lax.ppermute(x, "exp", swap_pairs)

    def trade_along(x, step):
        pairs = []
        for y in range(ring):
            for c in range(2):
                way = step if (y + c) % 2 == 0 else -step
                pairs.append((2 * y + c, 2 * ((y + way) % ring) + c))
        return lax.ppermute(x, "exp", pairs)

    width, count = tokens.shape[1], tokens.shape[0]
    slots = flight * HALF
    hidden, _ = down_weight_blocks.shape[1:]
    piece = 2 * width
    rank = adapter_up_matrix.shape[1]
    pad = up128(piece + rank)

    tok, cot = tokens.T, cotangent.T
    tok_far = swap(tok)
    cot_far = swap(cot)
    pick, weigh, one = call(
        assign, [((slots, count), BF)] * 3, where, expert_indices.T, routing_weights.T,
    )
    (rows,) = call(select_rows, [((slots, piece), BF)], where, one, tok, tok_far, local=(3,))
    (grads,) = call(
        select_grads, [((slots, piece), BF)], where, one, pick, weigh, cot, cot_far,
        local=(5,),
    )

    def trade(x):
        x = x.reshape(flight, HALF, piece)
        return lax.all_to_all(x, "ctx", split_axis=0, concat_axis=0, tiled=True).reshape(slots, piece)

    x0 = trade(rows)
    got_grads = trade(grads)

    (near,) = call(
        prepare,
        [((3 * ring + 1, up8(hidden), pad), BF)],
        gate_up_weight_blocks[0].transpose(1, 0, 2),
        gate_up_block_scales[0].transpose(1, 0, 2),
        down_weight_blocks[0],
        down_block_scales[0][:, None, :],
        adapter_down_matrix[0].T,
        adapter_up_matrix[0],
        scalars=0, keep=True,
    )
    far = swap(near)

    x1 = trade_along(x0, 1)
    (first,) = call(join, [((2 * slots, piece), BF)], x0, x1, scalars=0, keep=True, local=(1,))
    second = trade_along(first, -1)
    third = trade_along(second, 1)
    last = trade_along(third, -1)
    (sums,) = call(
        project_four, [((2, 2, slots, hidden), F32)], where, near, far, first, second, local=(1, 2, 3)
    )
    (sums,) = call(
        project_more, [((2, 2, slots, hidden), F32)], where, near, far, third, sums, local=(1, 2)
    )
    tall = slots + rank + 4
    act_near, act_far, up, partial = call(
        expert,
        [((slots, hidden), BF)] * 2 + [((rank, piece), BF), ((ring * tall, pad), BF)],
        where, near, far, sums, last, got_grads,
        local=(1, 2, 4),
        scratch=[pltpu.VMEM((ring * tall, pad), F32)],
    )
    groups = [[2 * y + c for y in range(ring)] for c in range(2)]
    total = lax.psum_scatter(
        partial, "exp", scatter_dimension=0, tiled=True, axis_index_groups=groups
    )
    (expert_rows,) = call(finish, [((slots, piece), BF)], total, up, scalars=0, local=(0,), free=(1,))
    returned = trade(expert_rows)
    left, right, ranks = call(
        gradients,
        [((rank, hidden), F32), ((rank, width), F32), ((2 * rank, count), F32)],
        where, total, act_near, act_far, got_grads,
        keep=True, local=(1,),
    )
    mine, send = call(
        combine,
        [((width, count), F32), ((up8(width) + 2 * rank, count), F32)],
        where, returned, pick, weigh, ranks,
        keep=True, local=(1, 4), free=(2, 3),
        scratch=[pltpu.VMEM((piece, count), F32)],
    )
    got = swap(send)
    moe, left, right = call(
        settle,
        [((width, count), BF), ((rank, hidden), F32), ((rank, width), F32)],
        mine, left, right, got,
        scalars=0, local=(0, 1, 2, 3),
    )
    return (moe.T, left.T[None], right[None])


def solution(mesh):
    placed = (
        P("ctx", "exp"),
        P("ctx", "exp"),
        P("ctx", None),
        P("ctx", None),
        P("ctx", None, "exp", None),
        P("ctx", None, "exp", None),
        P("ctx", "exp", None),
        P("ctx", "exp", None),
        P("ctx", "exp", None),
        P("ctx", None, "exp"),
    )
    return jax.shard_map(
        on_device,
        mesh=mesh,
        in_specs=placed,
        out_specs=(P("ctx", "exp"), P("ctx", "exp", None), P("ctx", None, "exp")),
        check_vma=False,
    )
```

```python
import jax
import jax.numpy as jnp
from jax import lax
from jax.experimental import pallas as pl
from jax.experimental.pallas import tpu as pltpu
from jax.sharding import PartitionSpec as P


CAP = 16
HALF = CAP // 2
ADAPTER_SCALE = 0.5
GLU_ALPHA = 1.702
CLAMP_LIMIT = 7.0
BF = jnp.bfloat16
F32 = jnp.float32


NN = (((1,), (0,)), ((), ()))
NT = (((1,), (1,)), ((), ()))
TN = (((0,), (0,)), ((), ()))

ORDER = (0, 1, -1, -2, 2, 3, -3, -4)


def dot(a, b, dims):
    return lax.dot_general(a, b, dims, preferred_element_type=F32)


def iota(shape, axis):
    return lax.broadcasted_iota(jnp.int32, shape, axis)


def up8(n):
    return -(-n // 8) * 8


def up128(n):
    return -(-n // 128) * 128


def call(body, out_shape, *args, scalars=1, keep=(), local=(), free=(), scratch=()):
    smem = pl.BlockSpec(memory_space=pltpu.SMEM)
    vmem = pl.BlockSpec(memory_space=pltpu.VMEM)
    args = [
        x
        if i < scalars or i in free
        else pltpu.with_memory_space_constraint(x, pltpu.VMEM if i in local else pltpu.HBM)
        for i, x in enumerate(args)
    ]
    return pl.pallas_call(
        body,
        out_shape=[
            (pltpu.VMEM if keep is True or i in keep else pltpu.HBM)(dims, kind)
            for i, (dims, kind) in enumerate(out_shape)
        ],
        in_specs=[smem if i < scalars else vmem for i in range(len(args))],
        out_specs=[vmem for _ in out_shape],
        scratch_shapes=list(scratch),
        compiler_params=pltpu.CompilerParams(vmem_limit_bytes=24 << 20),
    )(*args)


def assign(where, ids, weights, pick, weigh, one, again):
    side = where[1]
    slots, count = pick.shape
    flight = slots // HALF
    named = jnp.zeros((flight, count), F32)
    weight = jnp.zeros((flight, count), F32)
    for k in range(ids.shape[0]):
        hit = ids[k : k + 1, :] == iota((flight, count), 0)
        named = named + jnp.where(hit, 1.0, 0.0)
        weight = weight + jnp.where(hit, weights[k : k + 1, :], 0.0)
    earlier = jnp.where(iota((count, count), 0) < iota((count, count), 1), 1.0, 0.0).astype(BF)
    before = dot(named.astype(BF), earlier, NN) - (side * HALF).astype(F32)
    slot = iota((flight, HALF, count), 1).astype(F32)
    taken = (before[:, None, :] == slot) & (named[:, None, :] > 0.5)
    chosen = jnp.where(taken, 1.0, 0.0).reshape(slots, count).astype(BF)
    one[...] = chosen
    again[...] = chosen
    scaled = jnp.where(taken, weight[:, None, :], 0.0).reshape(slots, count)
    upper = scaled.astype(BF)
    pick[...] = upper
    weigh[...] = (scaled - upper.astype(F32)).astype(BF)


def features(where, near, far, second):
    side = where[1]
    both = near.shape[0]
    width = both // 2
    row, col = iota((both, both), 0), iota((both, both), 1)
    inside = (col >= width) if second else (col < width)
    at = row + width if second else row
    left = jnp.where((at == col + side * width) & inside, 1.0, 0.0).astype(BF)
    right = jnp.where((at == col + (1 - side) * width) & inside, 1.0, 0.0).astype(BF)
    return (dot(left, near[...], NN) + dot(right, far[...], NN)).astype(BF)


def select_rows(where, one, near, far, rows):
    rows[...] = dot(one[...], features(where, near, far, False), NT).astype(BF)


def select_grads(where, one, pick, weigh, near, far, grads):
    factor = jnp.sum(pick[...].astype(F32) + weigh[...].astype(F32), axis=1, keepdims=True)
    grads[...] = (factor * dot(one[...], features(where, near, far, True), NT)).astype(BF)


def join(first, second, out):
    count = first.shape[0]
    out[:count, :] = first[...]
    out[count:, :] = second[...]


def prepare(joined, joined_scales, down, down_scales, left, up, out):
    hidden, width = down.shape
    groups = down_scales.shape[2]
    group = width // groups
    parts = len(ORDER)
    piece = width // parts
    rank = left.shape[0]
    pad = out.shape[2]
    spread = jnp.where(
        iota((groups, width), 1) // group == iota((groups, width), 0), 1.0, 0.0
    ).astype(BF)

    def scaled(codes, scales):
        upper = scales.astype(BF)
        lower = (scales - upper.astype(F32)).astype(BF)
        return codes.astype(F32) * (dot(upper, spread, NN) + dot(lower, spread, NN))

    for c in range(2):
        full = scaled(joined[:, c, :], joined_scales[:, c, :])
        for a in range(parts):
            out[2 * a + c, :hidden, :piece] = full[:, a * piece : (a + 1) * piece].astype(BF)
    full = scaled(down[...], down_scales[:, 0, :])
    shifted = jnp.where(iota((rank, pad), 1) == iota((rank, pad), 0) + piece, 1.0, 0.0).astype(BF)
    added = dot(left[...], shifted, TN).astype(BF)
    for a in range(parts):
        out[2 * parts + a, :hidden, :] = added
        out[2 * parts + a, :hidden, :piece] = full[:, a * piece : (a + 1) * piece].astype(BF)
    out[3 * parts, :rank, : up.shape[1]] = up[...]


def source(where, q):
    parts = len(ORDER)
    return lax.rem(where[0] + where[2] * ORDER[q] + parts, parts)


def project_into(where, first, near, far, blocks, before, sums):
    hidden, count = sums.shape[3], sums.shape[2]
    piece = blocks[0].shape[1]
    spans = [(x, h * count) for x in blocks for h in range(2)]
    for n, weights in enumerate((near, far)):
        for c in range(2):
            acc = jnp.zeros((count, hidden), F32) if before is None else before[n, c]
            for q, (x, at) in enumerate(spans):
                part = weights[2 * source(where, first + q) + c, :hidden, :piece]
                acc = acc + dot(x[at : at + count, :], part, NT)
            sums[n, c] = acc


def project_four(where, near, far, first, second, sums):
    project_into(where, 0, near, far, (first, second), None, sums)


def project_more(where, near, far, third, before, sums):
    project_into(where, 4, near, far, (third,), before, sums)


def expert(where, near, far, sums, last, grads, act_near, act_far, up, out, wide):
    side = where[1]
    count, hidden = act_near.shape
    piece = last.shape[1]
    parts = len(ORDER)
    rank = up.shape[0]
    half = piece // 2
    tall = out.shape[0] // parts
    pad = out.shape[1]
    acts = []
    for n, (weights, act) in enumerate(((near, act_near), (far, act_far))):
        total = []
        for c in range(2):
            acc = sums[n, c]
            for h in range(2):
                part = weights[2 * source(where, parts - 2 + h) + c, :hidden, :piece]
                acc = acc + dot(last[h * count : (h + 1) * count, :], part, NT)
            total.append(acc)
        gate = jnp.minimum(total[0], CLAMP_LIMIT)
        lift = jnp.clip(total[1], -CLAMP_LIMIT, CLAMP_LIMIT)
        value = ((lift + 1.0) * gate * jax.nn.sigmoid(GLU_ALPHA * gate)).astype(BF)
        act[...] = value
        acts.append(value)
    row, col = iota((half, piece), 0), iota((half, piece), 1)
    here = jnp.where(row + side * half == col, 1.0, 0.0).astype(BF)
    there = jnp.where(row + (1 - side) * half == col, 1.0, 0.0).astype(BF)
    both = dot(near[3 * parts, :rank, :half], here, NN) + dot(far[3 * parts, :rank, :half], there, NN)
    both = both.astype(BF)
    up[...] = both
    few = rank // 2
    free = pad - few
    spread = jnp.where(
        iota((pad, rank), 0) - free == iota((pad, rank), 1) - few, 1.0, 0.0
    ) * jnp.where(iota((pad, rank), 0) >= free, 1.0, 0.0)
    beside = dot(grads[...], dot(spread.astype(BF), both, NN).astype(BF), NT)
    back = dot(both, grads[...], NT)[:few]
    for a in range(parts):
        total = dot(acts[0], near[2 * parts + a, :hidden, :], NN) + dot(acts[1], far[2 * parts + a, :hidden, :], NN)
        wide[a * tall : a * tall + count, :] = total + beside
        wide[a * tall + count : (a + 1) * tall, :] = jnp.zeros((tall - count, pad), F32)
        wide[a * tall + count : a * tall + count + few, :count] = back
    out[...] = wide[...].astype(BF)


def finish(total, up, out):
    count, piece = out.shape
    pad = total.shape[1]
    rank = up.shape[0]
    lift = jnp.where(iota((pad, rank), 0) == iota((pad, rank), 1) + piece, 1.0, 0.0).astype(BF)
    low = dot(total[:count, :], lift, NN).astype(BF)
    added = ADAPTER_SCALE * dot(low, up[...], NN)
    out[...] = (total[:count, :piece].astype(F32) + added).astype(BF)


def gradients(where, total, act_near, act_far, grads, left, right, send):
    side = where[1]
    count, piece = grads.shape
    rank, half = left.shape
    few = rank // 2
    free = total.shape[1] - few
    back = total[count : count + few, :count]
    send[...] = jnp.zeros(send.shape, F32)
    for act, at in ((act_near, left), (act_far, send)):
        at[:few, :half] = ADAPTER_SCALE * dot(back, act[...], NN)
        at[few:rank, :half] = ADAPTER_SCALE * dot(total[:count, :], act[...], TN)[free:]
    product = dot(total[:count, :], grads[...], TN)
    whole = ADAPTER_SCALE * product[piece : piece + rank]
    first, second = whole[:, :half], whole[:, half:]
    right[...] = jnp.where(side == 0, first, second)
    send[rank:, :half] = jnp.where(side == 0, second, first)


def combine(where, returned, pick, weigh, ranks, mine, send, whole):
    side = where[1]
    half = mine.shape[0]
    whole[...] = dot(returned[...], pick[...], TN) + dot(returned[...], weigh[...], TN)
    first, second = whole[:half, :], whole[half:, :]
    mine[...] = jnp.where(side == 0, first, second)
    send[:half, :] = jnp.where(side == 0, second, first)
    start = send.shape[0] - ranks.shape[0]
    send[start:, :] = ranks[...]


def settle(mine, left, right, got, out, left_out, right_out):
    half = mine.shape[0]
    rank, wide = left.shape
    start = got.shape[0] - 2 * rank
    out[...] = (mine[...] + got[:half, :]).astype(BF)
    left_out[...] = left[...] + got[start : start + rank, :wide]
    right_out[...] = right[...] + got[start + rank :, :wide]


def on_device(
    tokens,
    cotangent,
    expert_indices,
    routing_weights,
    gate_up_weight_blocks,
    gate_up_block_scales,
    down_weight_blocks,
    down_block_scales,
    adapter_down_matrix,
    adapter_up_matrix,
):
    flight = lax.axis_size("ctx")
    peers = lax.axis_size("exp")
    ring = peers // 2
    index = lax.axis_index("exp")
    chip, side = index // 2, index % 2
    sign = 1 - 2 * ((chip + side) % 2)
    where = jnp.stack([chip, side, sign]).astype(jnp.int32)
    swap_pairs = [(i, i ^ 1) for i in range(peers)]

    def swap(x):
        return lax.ppermute(x, "exp", swap_pairs)

    def trade_along(x, step):
        pairs = []
        for y in range(ring):
            for c in range(2):
                way = step if (y + c) % 2 == 0 else -step
                pairs.append((2 * y + c, 2 * ((y + way) % ring) + c))
        return lax.ppermute(x, "exp", pairs)

    count, width = tokens.shape
    slots = flight * HALF
    hidden, _ = down_weight_blocks.shape[1:]
    piece = 2 * width
    rank = adapter_up_matrix.shape[1]
    pad = up128(piece + rank)

    own = jnp.concatenate([tokens.T, cotangent.T], axis=0)
    other = swap(own)
    pick, weigh, one, again = call(
        assign, [((slots, count), BF)] * 4, where, expert_indices.T, routing_weights.T,
        keep=(2,),
    )
    (rows,) = call(
        select_rows, [((slots, piece), BF)], where, one, own, other, local=(1, 2, 3)
    )
    (grads,) = call(
        select_grads, [((slots, piece), BF)], where, again, pick, weigh, own, other
    )

    def trade(x):
        x = x.reshape(flight, HALF, piece)
        return lax.all_to_all(x, "ctx", split_axis=0, concat_axis=0, tiled=True).reshape(slots, piece)

    x0 = trade(rows)
    got_grads = trade(grads)

    (near,) = call(
        prepare,
        [((3 * ring + 1, up8(hidden), pad), BF)],
        gate_up_weight_blocks[0].transpose(1, 0, 2),
        gate_up_block_scales[0].transpose(1, 0, 2),
        down_weight_blocks[0],
        down_block_scales[0][:, None, :],
        adapter_down_matrix[0].T,
        adapter_up_matrix[0],
        scalars=0, keep=True,
    )
    far = swap(near)

    x1 = trade_along(x0, 1)
    (first,) = call(join, [((2 * slots, piece), BF)], x0, x1, scalars=0, keep=True, local=(1,))
    second = trade_along(first, -1)
    third = trade_along(second, 1)
    last = trade_along(third, -1)
    (sums,) = call(
        project_four, [((2, 2, slots, hidden), F32)], where, near, far, first, second, local=(1, 2, 3)
    )
    (sums,) = call(
        project_more, [((2, 2, slots, hidden), F32)], where, near, far, third, sums, local=(1, 2)
    )
    tall = slots + rank // 2 + 4
    act_near, act_far, up, partial = call(
        expert,
        [((slots, hidden), BF)] * 2 + [((rank, piece), BF), ((ring * tall, pad), BF)],
        where, near, far, sums, last, got_grads,
        local=(1, 2, 4),
        scratch=[pltpu.VMEM((ring * tall, pad), F32)],
    )
    groups = [[2 * y + c for y in range(ring)] for c in range(2)]
    total = lax.psum_scatter(
        partial, "exp", scatter_dimension=0, tiled=True, axis_index_groups=groups
    )
    (expert_rows,) = call(finish, [((slots, piece), BF)], total, up, scalars=0, local=(0,), free=(1,))
    returned = trade(expert_rows)
    left, right, ranks = call(
        gradients,
        [((rank, hidden), F32), ((rank, width), F32), ((2 * rank, count), F32)],
        where, total, act_near, act_far, got_grads,
        keep=True, local=(1,),
    )
    mine, send = call(
        combine,
        [((width, count), F32), ((up8(width) + 2 * rank, count), F32)],
        where, returned, pick, weigh, ranks,
        keep=True, local=(1, 4), free=(2, 3),
        scratch=[pltpu.VMEM((piece, count), F32)],
    )
    got = swap(send)
    moe, left, right = call(
        settle,
        [((width, count), BF), ((rank, hidden), F32), ((rank, width), F32)],
        mine, left, right, got,
        scalars=0, local=(0, 1, 2, 3),
    )
    return (moe.T, left.T[None], right[None])


def solution(mesh):
    placed = (
        P("ctx", "exp"),
        P("ctx", "exp"),
        P("ctx", None),
        P("ctx", None),
        P("ctx", None, "exp", None),
        P("ctx", None, "exp", None),
        P("ctx", "exp", None),
        P("ctx", "exp", None),
        P("ctx", "exp", None),
        P("ctx", None, "exp"),
    )
    return jax.shard_map(
        on_device,
        mesh=mesh,
        in_specs=placed,
        out_specs=(P("ctx", "exp"), P("ctx", "exp", None), P("ctx", None, "exp")),
        check_vma=False,
    )
```

```python
import jax
import jax.numpy as jnp
from jax import lax
from jax.experimental import pallas as pl
from jax.experimental.pallas import tpu as pltpu
from jax.sharding import PartitionSpec as P


CAP = 16
HALF = CAP // 2
ADAPTER_SCALE = 0.5
GLU_ALPHA = 1.702
CLAMP_LIMIT = 7.0
BF = jnp.bfloat16
F32 = jnp.float32


NN = (((1,), (0,)), ((), ()))
NT = (((1,), (1,)), ((), ()))
TN = (((0,), (0,)), ((), ()))

ORDER = (0, 1, -1, -2, 2, 3, -3, -4)


def dot(a, b, dims):
    return lax.dot_general(a, b, dims, preferred_element_type=F32)


def iota(shape, axis):
    return lax.broadcasted_iota(jnp.int32, shape, axis)


def up8(n):
    return -(-n // 8) * 8


def up128(n):
    return -(-n // 128) * 128


def call(body, out_shape, *args, scalars=1, keep=(), local=(), free=(), scratch=()):
    smem = pl.BlockSpec(memory_space=pltpu.SMEM)
    vmem = pl.BlockSpec(memory_space=pltpu.VMEM)
    args = [
        x
        if i < scalars or i in free
        else pltpu.with_memory_space_constraint(x, pltpu.VMEM if i in local else pltpu.HBM)
        for i, x in enumerate(args)
    ]
    return pl.pallas_call(
        body,
        out_shape=[
            (pltpu.VMEM if keep is True or i in keep else pltpu.HBM)(dims, kind)
            for i, (dims, kind) in enumerate(out_shape)
        ],
        in_specs=[smem if i < scalars else vmem for i in range(len(args))],
        out_specs=[vmem for _ in out_shape],
        scratch_shapes=list(scratch),
        compiler_params=pltpu.CompilerParams(vmem_limit_bytes=24 << 20),
    )(*args)


def assign(where, ids, weights, pick, weigh, one, again):
    side = where[1]
    slots, count = pick.shape
    flight = slots // HALF
    named = jnp.zeros((flight, count), F32)
    weight = jnp.zeros((flight, count), F32)
    for k in range(ids.shape[0]):
        hit = ids[k : k + 1, :] == iota((flight, count), 0)
        named = named + jnp.where(hit, 1.0, 0.0)
        weight = weight + jnp.where(hit, weights[k : k + 1, :], 0.0)
    earlier = jnp.where(iota((count, count), 0) < iota((count, count), 1), 1.0, 0.0).astype(BF)
    before = dot(named.astype(BF), earlier, NN) - (side * HALF).astype(F32)
    slot = iota((flight, HALF, count), 1).astype(F32)
    taken = (before[:, None, :] == slot) & (named[:, None, :] > 0.5)
    chosen = jnp.where(taken, 1.0, 0.0).reshape(slots, count).astype(BF)
    one[...] = chosen
    again[...] = chosen
    scaled = jnp.where(taken, weight[:, None, :], 0.0).reshape(slots, count)
    upper = scaled.astype(BF)
    pick[...] = upper
    weigh[...] = (scaled - upper.astype(F32)).astype(BF)


def features(where, near, far, second):
    side = where[1]
    both = near.shape[0]
    width = both // 2
    row, col = iota((both, both), 0), iota((both, both), 1)
    inside = (col >= width) if second else (col < width)
    at = row + width if second else row
    left = jnp.where((at == col + side * width) & inside, 1.0, 0.0).astype(BF)
    right = jnp.where((at == col + (1 - side) * width) & inside, 1.0, 0.0).astype(BF)
    return (dot(left, near[...], NN) + dot(right, far[...], NN)).astype(BF)


def select_rows(where, one, near, far, rows):
    rows[...] = dot(one[...], features(where, near, far, False), NT).astype(BF)


def select_grads(where, one, pick, weigh, near, far, grads):
    factor = jnp.sum(pick[...].astype(F32) + weigh[...].astype(F32), axis=1, keepdims=True)
    grads[...] = (factor * dot(one[...], features(where, near, far, True), NT)).astype(BF)


def join(first, second, out):
    count = first.shape[0]
    out[:count, :] = first[...]
    out[count:, :] = second[...]


def prepare(joined, joined_scales, down, down_scales, left, up, out):
    hidden, width = down.shape
    groups = down_scales.shape[2]
    group = width // groups
    parts = len(ORDER)
    piece = width // parts
    rank = left.shape[0]
    pad = out.shape[2]
    spread = jnp.where(
        iota((groups, width), 1) // group == iota((groups, width), 0), 1.0, 0.0
    ).astype(BF)

    def scaled(codes, scales):
        upper = scales.astype(BF)
        lower = (scales - upper.astype(F32)).astype(BF)
        return codes.astype(F32) * (dot(upper, spread, NN) + dot(lower, spread, NN))

    for c in range(2):
        full = scaled(joined[:, c, :], joined_scales[:, c, :])
        for a in range(parts):
            out[2 * a + c, :hidden, :piece] = full[:, a * piece : (a + 1) * piece].astype(BF)
    full = scaled(down[...], down_scales[:, 0, :])
    shifted = jnp.where(iota((rank, pad), 1) == iota((rank, pad), 0) + piece, 1.0, 0.0).astype(BF)
    added = dot(left[...], shifted, TN).astype(BF)
    for a in range(parts):
        out[2 * parts + a, :hidden, :] = added
        out[2 * parts + a, :hidden, :piece] = full[:, a * piece : (a + 1) * piece].astype(BF)
    out[3 * parts, :rank, : up.shape[1]] = up[...]


def source(where, q):
    parts = len(ORDER)
    return lax.rem(where[0] + where[2] * ORDER[q] + parts, parts)


def pick_call(body, out_shape, where, picked, *args, local=(), scratch=()):
    near, far, blocks = picked
    near, far, *args = [
        pltpu.with_memory_space_constraint(x, pltpu.VMEM if any(x is y for y in local) else pltpu.HBM)
        for x in (near, far, *args)
    ]
    specs = []
    for _ in range(2):
        for rows, place in blocks:
            specs.append(
                pl.BlockSpec((rows,) + near.shape[1:], lambda i, w, place=place: (place(w), 0, 0))
            )
    whole = lambda dims: pl.BlockSpec(dims, lambda i, w, n=len(dims): (0,) * n)
    return pl.pallas_call(
        body,
        out_shape=[pltpu.HBM(dims, kind) for dims, kind in out_shape],
        grid_spec=pltpu.PrefetchScalarGridSpec(
            num_scalar_prefetch=1,
            grid=(1,),
            in_specs=specs + [whole(x.shape) for x in args],
            out_specs=[whole(dims) for dims, _ in out_shape],
            scratch_shapes=list(scratch),
        ),
        compiler_params=pltpu.CompilerParams(vmem_limit_bytes=32 << 20),
    )(where, *([near] * len(blocks)), *([far] * len(blocks)), *args)


def project_into(weights, blocks, before, sums):
    hidden, count = sums.shape[3], sums.shape[2]
    piece = blocks[0].shape[1]
    spans = [(x, h * count) for x in blocks for h in range(2)]
    for n in range(2):
        for c in range(2):
            acc = jnp.zeros((count, hidden), F32) if before is None else before[n, c]
            for q, (x, at) in enumerate(spans):
                part = weights[n * len(spans) + q][c, :hidden, :piece]
                acc = acc + dot(x[at : at + count, :], part, NT)
            sums[n, c] = acc


def project_four(where, a, b, c, d, e, f, g, h, first, second, sums):
    project_into((a, b, c, d, e, f, g, h), (first, second), None, sums)


def project_more(where, a, b, c, d, third, before, sums):
    project_into((a, b, c, d), (third,), before, sums)


def expert(
    where, near_a, near_b, near_down, near_up, far_a, far_b, far_down, far_up,
    sums, last, grads, act_near, act_far, up, out, wide,
):
    side = where[1]
    count, hidden = act_near.shape
    piece = last.shape[1]
    parts = len(ORDER)
    rank = up.shape[0]
    half = piece // 2
    tall = out.shape[0] // parts
    pad = out.shape[1]
    acts = []
    for n, (weights, act) in enumerate((((near_a, near_b), act_near), ((far_a, far_b), act_far))):
        total = []
        for c in range(2):
            acc = sums[n, c]
            for h in range(2):
                part = weights[h][c, :hidden, :piece]
                acc = acc + dot(last[h * count : (h + 1) * count, :], part, NT)
            total.append(acc)
        gate = jnp.minimum(total[0], CLAMP_LIMIT)
        lift = jnp.clip(total[1], -CLAMP_LIMIT, CLAMP_LIMIT)
        value = ((lift + 1.0) * gate * jax.nn.sigmoid(GLU_ALPHA * gate)).astype(BF)
        act[...] = value
        acts.append(value)
    row, col = iota((half, piece), 0), iota((half, piece), 1)
    here = jnp.where(row + side * half == col, 1.0, 0.0).astype(BF)
    there = jnp.where(row + (1 - side) * half == col, 1.0, 0.0).astype(BF)
    both = dot(near_up[0, :rank, :half], here, NN) + dot(far_up[0, :rank, :half], there, NN)
    both = both.astype(BF)
    up[...] = both
    few = rank // 2
    free = pad - few
    spread = jnp.where(
        iota((pad, rank), 0) - free == iota((pad, rank), 1) - few, 1.0, 0.0
    ) * jnp.where(iota((pad, rank), 0) >= free, 1.0, 0.0)
    beside = dot(grads[...], dot(spread.astype(BF), both, NN).astype(BF), NT)
    back = dot(both, grads[...], NT)[:few]
    for a in range(parts):
        total = dot(acts[0], near_down[a, :hidden, :], NN) + dot(acts[1], far_down[a, :hidden, :], NN)
        wide[a * tall : a * tall + count, :] = total + beside
        wide[a * tall + count : (a + 1) * tall, :] = jnp.zeros((tall - count, pad), F32)
        wide[a * tall + count : a * tall + count + few, :count] = back
    out[...] = wide[...].astype(BF)


def finish(total, up, out):
    count, piece = out.shape
    pad = total.shape[1]
    rank = up.shape[0]
    lift = jnp.where(iota((pad, rank), 0) == iota((pad, rank), 1) + piece, 1.0, 0.0).astype(BF)
    low = dot(total[:count, :], lift, NN).astype(BF)
    added = ADAPTER_SCALE * dot(low, up[...], NN)
    out[...] = (total[:count, :piece].astype(F32) + added).astype(BF)


def gradients(where, total, act_near, act_far, grads, left, right, send):
    side = where[1]
    count, piece = grads.shape
    rank, half = left.shape
    few = rank // 2
    free = total.shape[1] - few
    back = total[count : count + few, :count]
    send[...] = jnp.zeros(send.shape, F32)
    for act, at in ((act_near, left), (act_far, send)):
        at[:few, :half] = ADAPTER_SCALE * dot(back, act[...], NN)
        at[few:rank, :half] = ADAPTER_SCALE * dot(total[:count, :], act[...], TN)[free:]
    product = dot(total[:count, :], grads[...], TN)
    whole = ADAPTER_SCALE * product[piece : piece + rank]
    first, second = whole[:, :half], whole[:, half:]
    right[...] = jnp.where(side == 0, first, second)
    send[rank:, :half] = jnp.where(side == 0, second, first)


def combine(where, returned, pick, weigh, ranks, mine, send, whole):
    side = where[1]
    half = mine.shape[0]
    whole[...] = dot(returned[...], pick[...], TN) + dot(returned[...], weigh[...], TN)
    first, second = whole[:half, :], whole[half:, :]
    mine[...] = jnp.where(side == 0, first, second)
    send[:half, :] = jnp.where(side == 0, second, first)
    start = send.shape[0] - ranks.shape[0]
    send[start:, :] = ranks[...]


def settle(mine, left, right, got, out, left_out, right_out):
    half = mine.shape[0]
    rank, wide = left.shape
    start = got.shape[0] - 2 * rank
    out[...] = (mine[...] + got[:half, :]).astype(BF)
    left_out[...] = left[...] + got[start : start + rank, :wide]
    right_out[...] = right[...] + got[start + rank :, :wide]


def on_device(
    tokens,
    cotangent,
    expert_indices,
    routing_weights,
    gate_up_weight_blocks,
    gate_up_block_scales,
    down_weight_blocks,
    down_block_scales,
    adapter_down_matrix,
    adapter_up_matrix,
):
    flight = lax.axis_size("ctx")
    peers = lax.axis_size("exp")
    ring = peers // 2
    index = lax.axis_index("exp")
    chip, side = index // 2, index % 2
    sign = 1 - 2 * ((chip + side) % 2)
    where = jnp.stack([chip, side, sign]).astype(jnp.int32)
    swap_pairs = [(i, i ^ 1) for i in range(peers)]

    def swap(x):
        return lax.ppermute(x, "exp", swap_pairs)

    def trade_along(x, step):
        pairs = []
        for y in range(ring):
            for c in range(2):
                way = step if (y + c) % 2 == 0 else -step
                pairs.append((2 * y + c, 2 * ((y + way) % ring) + c))
        return lax.ppermute(x, "exp", pairs)

    count, width = tokens.shape
    slots = flight * HALF
    hidden, _ = down_weight_blocks.shape[1:]
    piece = 2 * width
    rank = adapter_up_matrix.shape[1]
    pad = up128(piece + rank)

    own = jnp.concatenate([tokens.T, cotangent.T], axis=0)
    other = swap(own)
    pick, weigh, one, again = call(
        assign, [((slots, count), BF)] * 4, where, expert_indices.T, routing_weights.T,
        keep=(2,),
    )
    (rows,) = call(
        select_rows, [((slots, piece), BF)], where, one, own, other, local=(1, 2, 3)
    )
    (grads,) = call(
        select_grads, [((slots, piece), BF)], where, again, pick, weigh, own, other
    )

    def trade(x):
        x = x.reshape(flight, HALF, piece)
        return lax.all_to_all(x, "ctx", split_axis=0, concat_axis=0, tiled=True).reshape(slots, piece)

    x0 = trade(rows)
    got_grads = trade(grads)

    (near,) = call(
        prepare,
        [((3 * ring + 1, up8(hidden), pad), BF)],
        gate_up_weight_blocks[0].transpose(1, 0, 2),
        gate_up_block_scales[0].transpose(1, 0, 2),
        down_weight_blocks[0],
        down_block_scales[0][:, None, :],
        adapter_down_matrix[0].T,
        adapter_up_matrix[0],
        scalars=0,
    )
    far = swap(near)

    x1 = trade_along(x0, 1)
    (first,) = call(join, [((2 * slots, piece), BF)], x0, x1, scalars=0, keep=True, local=(0, 1))
    second = trade_along(first, -1)
    third = trade_along(second, 1)
    last = trade_along(third, -1)

    def arriving(begin, end):
        return [(2, lambda w, q=q: source(w, q)) for q in range(begin, end)]

    (sums,) = pick_call(
        project_four, [((2, 2, slots, hidden), F32)],
        where, (near, far, arriving(0, 4)), first, second, local=(first, second),
    )
    (sums,) = pick_call(
        project_more, [((2, 2, slots, hidden), F32)],
        where, (near, far, arriving(4, 6)), third, sums, local=(third,),
    )
    tall = slots + rank // 2 + 4
    act_near, act_far, up, partial = pick_call(
        expert,
        [((slots, hidden), BF)] * 2 + [((rank, piece), BF), ((ring * tall, pad), BF)],
        where,
        (near, far, arriving(6, 8) + [(ring, lambda w: 2), (1, lambda w: 3 * ring)]),
        sums, last, got_grads,
        local=(last, got_grads),
        scratch=[pltpu.VMEM((ring * tall, pad), F32)],
    )
    groups = [[2 * y + c for y in range(ring)] for c in range(2)]
    total = lax.psum_scatter(
        partial, "exp", scatter_dimension=0, tiled=True, axis_index_groups=groups
    )
    (expert_rows,) = call(finish, [((slots, piece), BF)], total, up, scalars=0, local=(0,), free=(1,))
    returned = trade(expert_rows)
    left, right, ranks = call(
        gradients,
        [((rank, hidden), F32), ((rank, width), F32), ((2 * rank, count), F32)],
        where, total, act_near, act_far, got_grads,
        keep=True, local=(1,), free=(2, 3, 4),
    )
    mine, send = call(
        combine,
        [((width, count), F32), ((up8(width) + 2 * rank, count), F32)],
        where, returned, pick, weigh, ranks,
        keep=True, local=(1, 4), free=(2, 3),
        scratch=[pltpu.VMEM((piece, count), F32)],
    )
    got = swap(send)
    moe, left, right = call(
        settle,
        [((width, count), BF), ((rank, hidden), F32), ((rank, width), F32)],
        mine, left, right, got,
        scalars=0, local=(0, 1, 2, 3),
    )
    return (moe.T, left.T[None], right[None])


def solution(mesh):
    placed = (
        P("ctx", "exp"),
        P("ctx", "exp"),
        P("ctx", None),
        P("ctx", None),
        P("ctx", None, "exp", None),
        P("ctx", None, "exp", None),
        P("ctx", "exp", None),
        P("ctx", "exp", None),
        P("ctx", "exp", None),
        P("ctx", None, "exp"),
    )
    return jax.shard_map(
        on_device,
        mesh=mesh,
        in_specs=placed,
        out_specs=(P("ctx", "exp"), P("ctx", "exp", None), P("ctx", None, "exp")),
        check_vma=False,
    )
```
